512 devices in a mesh: group: 64 (over x, z_lo, y), shard: 8 (over z_hi, core).
Axes of the slice: x: 4, y: 8, z: 8 (z_hi: 4, z_lo: 2; z = z_hi * 2 + z_lo), core: 2. Of those that a mesh axis runs over, the one named last changes fastest.
Arguments:
- owners: int32 [6], replicated, may hold values from 0 to 7, as said below
- mat_weight: bfloat16 [6, 128, 4096], P(None, 'shard'), may hold values from -0.09375 to 0.09375
- mat_grad: bfloat16 [64, 6, 128, 4096], P('group', None, 'shard'), may hold values from -2 to 2
- head_block_momentum: bfloat16 [6, 128, 4096], P(None, 'shard'), may hold values from -48 to 48
- emb_weight: bfloat16 [256, 4096], P('shard'), may hold values from -6 to 6
- emb_grad: bfloat16 [64, 256, 4096], P('group', 'shard'), may hold values from -2 to 2
- emb_first: float32 [256, 4096], P('shard'), may hold values from -6 to 6
- emb_second: float32 [256, 4096], P('shard'), may hold values from 0.1 to 10
- norm_weight: bfloat16 [2, 4096], P(None, 'shard'), may hold values from 0.5 to 1.5
- norm_grad: bfloat16 [64, 2, 4096], P('group', None, 'shard'), may hold values from -2 to 2
- norm_first: float32 [2, 4096], P(None, 'shard'), may hold values from -6 to 6
- norm_second: float32 [2, 4096], P(None, 'shard'), may hold values from 0.1 to 10
- qk_weight: bfloat16 [2, 128], replicated, may hold values from 0.5 to 1.5
- qk_grad: bfloat16 [64, 2, 128], P('group'), may hold values from -2 to 2
- qk_first: float32 [2, 128], replicated, may hold values from -6 to 6
- qk_second: float32 [2, 128], replicated, may hold values from 0.1 to 10
Outputs:
- new_weight: bfloat16 [6, 128, 4096], P(None, 'shard')
- new_moment: bfloat16 [6, 128, 4096], P(None, 'shard')
- owner_sums: float32 [8, 1], P('shard')
- emb_new: bfloat16 [256, 4096], P('shard')
- emb_first_new: float32 [256, 4096], P('shard')
- emb_second_new: float32 [256, 4096], P('shard')
- norm_new: bfloat16 [2, 4096], P(None, 'shard')
- norm_first_new: float32 [2, 4096], P(None, 'shard')
- norm_second_new: float32 [2, 4096], P(None, 'shard')
- qk_new: bfloat16 [2, 128], replicated
- qk_first_new: float32 [2, 128], replicated
- qk_second_new: float32 [2, 128], replicated
The draws below stay inside these ranges and needn't reach their ends.
Inputs may be any that keep to these rules, and one draw needn't show every extreme that they name: `owners`: each shard rank owns at most 1 head blocks, and some rank owns exactly 1.
All inputs are finite; a program needn't handle non-finite values.
Results may differ from the reference program's by a relative error of at most 0.008.
Values may be sent and summed in bfloat16 or wider, within the bound.
No kernel may reach another device: no remote copies, remote signals or barrier semaphores. Data moves between devices by JAX's collectives and lax.ppermute only.
A program may use at most 64 MiB of HBM per device.

```python
import math
import jax
import jax.numpy as jnp
from jax import lax

D = 4096
HEAD = 128
MATS = 6
NS_ITERS = 5
CAP = 1
EMB_ROWS = 256
N_GROUP = 64
N_SHARD = 8


def draw_owners(key, part):
    score_key = jax.random.fold_in(key, 11)
    order_key = jax.random.fold_in(key, 23)
    ranks = jnp.arange(N_SHARD, dtype=jnp.int32)
    scores = jax.random.randint(score_key, (N_SHARD,), 0, 1 << 20, dtype=jnp.int32) * N_SHARD + ranks
    scores = jnp.where(ranks == N_SHARD - 1, -2, jnp.where(ranks == 0, -1, scores))
    sequence = jnp.argsort(scores, stable=True).astype(jnp.int32)
    cyclic = sequence[jnp.arange(MATS) % N_SHARD]
    shuffled = jax.random.permutation(order_key, MATS)
    return cyclic[shuffled].astype(jnp.int32)


def draw_head_block_momentum(key, part):
    scale_key = jax.random.fold_in(key, 37)
    value_key = jax.random.fold_in(key, 41)
    spread = jax.random.uniform(scale_key, (MATS, 1, 1), jnp.float32, jnp.log(0.5), jnp.log(8.0))
    scales = jnp.exp(spread)
    values = jnp.clip(jax.random.normal(value_key, (MATS, HEAD, D), jnp.float32), -6.0, 6.0)
    return (values * scales).astype(jnp.bfloat16)


def block_scale(stream_key, dims, shards, low, top_value):
    loudness = 1.0
    for dim, shards_of in shards:
        draws = jax.random.uniform(jax.random.fold_in(jax.random.fold_in(stream_key, 6), dim), (shards_of,), jnp.float32, low / len(shards), top_value / len(shards))
        loudness = loudness * jnp.repeat(jnp.exp(draws), dims[dim] // shards_of).reshape((-1,) + (1,) * (len(dims) - 1 - dim))
    return loudness


def normal_values(own_key, extent, scale, most, split=(), kind=jnp.bfloat16):
    result = jax.random.normal(own_key, extent, jnp.float32) * scale
    if len(split) > 0:
        result = block_scale(own_key, extent, split, -0.22, 0.18) * result
    return jnp.clip(result, min=-most, max=most).astype(kind)


def setup_inputs(seed: int = 0) -> dict:
    streams_of = jax.random.split(jax.random.key(seed), 17)
    owners = draw_owners(jax.random.fold_in(streams_of[16], 71), 0)
    mat_weight = normal_values(streams_of[1], (MATS, HEAD, D), D ** -0.5, 0.09375, ((1, 8),))
    mat_grad = normal_values(streams_of[2], (N_GROUP, MATS, HEAD, D), 0.125, 2.0, ((0, 64), (2, 8)))
    head_block_momentum = draw_head_block_momentum(jax.random.fold_in(streams_of[16], 71), 0)
    emb_weight = normal_values(streams_of[4], (EMB_ROWS, D), 1.0, 6.0, ((0, 8),))
    emb_grad = normal_values(streams_of[5], (N_GROUP, EMB_ROWS, D), 0.125, 2.0, ((0, 64), (1, 8)))
    emb_first = normal_values(streams_of[6], (EMB_ROWS, D), 1.0, 6.0, ((0, 8),), jnp.float32)
    emb_second = jnp.clip(jnp.exp(math.log(10.0) - 4.6051702 * jax.random.uniform(streams_of[7], (EMB_ROWS, D), jnp.float32) ** block_scale(streams_of[7], (EMB_ROWS, D), ((0, 8),), -0.2, 0.2)), 0.1, 10.0)
    norm_weight = jnp.clip(1.0 + 0.1 * jax.random.normal(streams_of[8], (2, D), jnp.float32), 0.5, 1.5).astype(jnp.bfloat16)
    norm_grad = normal_values(streams_of[9], (N_GROUP, 2, D), 0.125, 2.0, ((0, 64), (2, 8)))
    norm_first = normal_values(streams_of[10], (2, D), 1.0, 6.0, ((1, 8),), jnp.float32)
    norm_second = jnp.clip(jnp.exp(math.log(10.0) - 4.6051702 * jax.random.uniform(streams_of[11], (2, D), jnp.float32) ** block_scale(streams_of[11], (2, D), ((1, 8),), -0.2, 0.2)), 0.1, 10.0)
    qk_weight = jnp.clip(1.0 + 0.1 * jax.random.normal(streams_of[12], (2, HEAD), jnp.float32), 0.5, 1.5).astype(jnp.bfloat16)
    qk_grad = normal_values(streams_of[13], (N_GROUP, 2, HEAD), 0.125, 2.0, ((0, 64),))
    qk_first = normal_values(streams_of[14], (2, HEAD), 1.0, 6.0, (), jnp.float32)
    qk_second = jnp.clip(jnp.exp(jax.random.uniform(streams_of[15], (2, HEAD), jnp.float32, math.log(0.1), math.log(10.0))), 0.1, 10.0)
    return dict(owners=owners, mat_weight=mat_weight, mat_grad=mat_grad, head_block_momentum=head_block_momentum, emb_weight=emb_weight, emb_grad=emb_grad, emb_first=emb_first, emb_second=emb_second, norm_weight=norm_weight, norm_grad=norm_grad, norm_first=norm_first, norm_second=norm_second, qk_weight=qk_weight, qk_grad=qk_grad, qk_first=qk_first, qk_second=qk_second)


momentum_decay = 0.95
muon_rate = 0.02
weight_decay = 0.1
adam_rate = 0.01
beta_first = 0.9
beta_second = 0.95
adam_epsilon = 1e-08
bias_first = 1.0 - 0.9 ** 10
bias_second = 1.0 - 0.95 ** 10
norm_epsilon = 1e-07
quintic_a = 3.4445
quintic_b = -4.775
quintic_c = 2.0315

def orthogonalize(matrix):
    widened = matrix.astype(jnp.float32)
    iterate = (widened / (jnp.sqrt(jnp.sum(widened * widened)) + norm_epsilon)).astype(jnp.bfloat16)
    for sweep in range(NS_ITERS):
        gram = jnp.dot(iterate, iterate.T, preferred_element_type=jnp.float32).astype(jnp.bfloat16)
        squared = jnp.dot(gram, gram, preferred_element_type=jnp.float32)
        blend = (quintic_b * gram.astype(jnp.float32) + quintic_c * squared).astype(jnp.bfloat16)
        iterate = (quintic_a * iterate.astype(jnp.float32) + jnp.dot(blend, iterate, preferred_element_type=jnp.float32)).astype(jnp.bfloat16)
    return iterate

def owner_slots(owners, capacity):
    order = jnp.arange(owners.shape[0], dtype=jnp.int32)
    same = (owners[:, None] == owners[None, :]) & (order[None, :] < order[:, None])
    position = lax.optimization_barrier(jnp.sum(same.astype(jnp.int32), axis=1))
    return owners * capacity + position

def adamw(weight, grad_sum, first, second):
    first_new = beta_first * first + (1.0 - beta_first) * grad_sum
    second_new = beta_second * second + (1.0 - beta_second) * grad_sum * grad_sum
    wide_weight = weight.astype(jnp.float32)
    stepped = first_new / bias_first / (jnp.sqrt(second_new / bias_second) + adam_epsilon) + weight_decay * wide_weight
    return ((wide_weight - adam_rate * stepped).astype(jnp.bfloat16), first_new, second_new)

def reference(owners, mat_weight, mat_grad, head_block_momentum, emb_weight, emb_grad, emb_first, emb_second, norm_weight, norm_grad, norm_first, norm_second, qk_weight, qk_grad, qk_first, qk_second):
    muon_scale = 0.2 * math.sqrt(max(HEAD, D))
    grad_total = lax.optimization_barrier(jnp.sum(mat_grad.astype(jnp.float32), axis=0))
    moment_wide = momentum_decay * head_block_momentum.astype(jnp.float32) + grad_total
    new_moment = moment_wide.astype(jnp.bfloat16)
    forwarded_rows = (grad_total + momentum_decay * moment_wide).astype(jnp.bfloat16)
    ortho = lax.map(orthogonalize, forwarded_rows)
    new_weight = (mat_weight.astype(jnp.float32) * (1.0 - muon_rate * weight_decay) - muon_rate * muon_scale * ortho.astype(jnp.float32)).astype(jnp.bfloat16)
    slots = owner_slots(owners, CAP)
    energy = lax.optimization_barrier(jnp.sum(ortho.astype(jnp.float32) * forwarded_rows.astype(jnp.float32), axis=(1, 2))) / (HEAD * math.sqrt(D))
    table = (slots[None, :] == jnp.arange(N_SHARD * CAP, dtype=jnp.int32)[:, None]).astype(jnp.float32)
    owner_sums = lax.optimization_barrier(jnp.sum(table * energy[None, :], axis=1)).reshape(N_SHARD, CAP)
    emb_new, emb_first_new, emb_second_new = adamw(emb_weight, lax.optimization_barrier(jnp.sum(emb_grad.astype(jnp.float32), axis=0)), emb_first, emb_second)
    norm_new, norm_first_new, norm_second_new = adamw(norm_weight, lax.optimization_barrier(jnp.sum(norm_grad.astype(jnp.float32), axis=0)), norm_first, norm_second)
    qk_new, qk_first_new, qk_second_new = adamw(qk_weight, lax.optimization_barrier(jnp.sum(qk_grad.astype(jnp.float32), axis=0)), qk_first, qk_second)
    return (new_weight, new_moment, owner_sums, emb_new, emb_first_new, emb_second_new, norm_new, norm_first_new, norm_second_new, qk_new, qk_first_new, qk_second_new)
```

```python
import math

import jax
import jax.numpy as jnp
from jax import lax
from jax.sharding import Mesh, PartitionSpec as P

D = 4096
HEAD = 128
MATS = 6
NS_ITERS = 5


momentum_decay = 0.95
muon_rate = 0.02
weight_decay = 0.1
adam_rate = 0.01
beta_first = 0.9
beta_second = 0.95
adam_epsilon = 1e-08
bias_first = 1.0 - 0.9**10
bias_second = 1.0 - 0.95**10
norm_epsilon = 1e-07
quintic_a = 3.4445
quintic_b = -4.775
quintic_c = 2.0315


COLUMNS = ("x", "z_lo")
SHARD = ("z_hi", "core")
SPARE = 8


def exchange(stacked, axes):
    return lax.all_to_all(stacked, axes, split_axis=0, concat_axis=0, tiled=True)


def spread(piece, axes):
    return exchange(jnp.broadcast_to(piece[None], (lax.axis_size(axes),) + piece.shape), axes)


def split_wide(wide):
    high = lax.reduce_precision(wide, 8, 7)
    low = lax.reduce_precision(wide - high, 8, 7)
    return high.astype(jnp.bfloat16), low.astype(jnp.bfloat16)


def orthogonalize(matrix):
    widened = matrix.astype(jnp.float32)
    iterate = (widened / (jnp.sqrt(jnp.sum(widened * widened)) + norm_epsilon)).astype(jnp.bfloat16)
    for sweep in range(NS_ITERS):
        gram = jnp.dot(iterate, iterate.T, preferred_element_type=jnp.float32).astype(jnp.bfloat16)
        squared = jnp.dot(gram, gram, preferred_element_type=jnp.float32)
        blend = (quintic_b * gram.astype(jnp.float32) + quintic_c * squared).astype(jnp.bfloat16)
        iterate = (
            quintic_a * iterate.astype(jnp.float32)
            + jnp.dot(blend, iterate, preferred_element_type=jnp.float32)
        ).astype(jnp.bfloat16)
    return iterate


def slot_energy(ortho, pushed):
    return jnp.sum(ortho.astype(jnp.float32) * pushed.astype(jnp.float32)) / (
        HEAD * math.sqrt(D)
    )


def owner_slots(owners, capacity):
    order = jnp.arange(owners.shape[0], dtype=jnp.int32)
    same = (owners[:, None] == owners[None, :]) & (order[None, :] < order[:, None])
    position = jnp.sum(same.astype(jnp.int32), axis=1)
    return owners * capacity + position


def adamw(weight, grad_sum, first, second):
    first_new = beta_first * first + (1.0 - beta_first) * grad_sum
    second_new = beta_second * second + (1.0 - beta_second) * grad_sum * grad_sum
    wide_weight = weight.astype(jnp.float32)
    stepped = (
        first_new / bias_first / (jnp.sqrt(second_new / bias_second) + adam_epsilon)
        + weight_decay * wide_weight
    )
    return ((wide_weight - adam_rate * stepped).astype(jnp.bfloat16), first_new, second_new)


def on_device(
    owners,
    mat_weight,
    mat_grad,
    head_block_momentum,
    emb_weight,
    emb_grad,
    emb_first,
    emb_second,
    norm_weight,
    norm_grad,
    norm_first,
    norm_second,
    qk_weight,
    qk_grad,
    qk_first,
    qk_second,
):
    muon_scale = 0.2 * math.sqrt(max(HEAD, D))
    mats, rows, width = mat_weight.shape
    blocks = lax.axis_size("y")
    pieces = lax.axis_size(COLUMNS)
    cols = width // pieces
    block = lax.axis_index("y")
    piece = lax.axis_index(COLUMNS)
    shard = lax.axis_index(SHARD)

    grads = jnp.concatenate(
        [mat_grad[0], emb_grad[0].reshape(blocks - mats, rows, width)], axis=0
    )
    grads = grads.reshape(blocks * rows, pieces, cols).transpose(1, 0, 2)
    gains = jnp.concatenate([norm_grad[0].reshape(-1), qk_grad[0].reshape(-1)])
    gains = jnp.pad(gains, (0, SPARE * cols - gains.shape[0])).reshape(1, SPARE, cols)
    outgoing = jnp.concatenate(
        [grads, jnp.broadcast_to(gains, (pieces, SPARE, cols))], axis=1
    )
    partial = jnp.sum(exchange(outgoing, COLUMNS).astype(jnp.float32), axis=0)

    gains_high, gains_low = split_wide(partial[blocks * rows : blocks * rows + SPARE // 2])
    gains = jnp.concatenate([gains_high, gains_low], axis=0)
    outgoing = jnp.concatenate(
        [
            partial[: blocks * rows].astype(jnp.bfloat16).reshape(blocks, rows, cols),
            jnp.broadcast_to(gains[None], (blocks, SPARE, cols)),
        ],
        axis=1,
    )
    total = jnp.sum(exchange(outgoing, "y").astype(jnp.float32), axis=0)
    grad_total = total[:rows]
    gains = total[rows : rows + SPARE // 2] + total[rows + SPARE // 2 :]
    gains = gains.reshape(-1)
    norm_total = gains[: norm_weight.size].reshape(norm_weight.shape)
    qk_total = gains[norm_weight.size : norm_weight.size + qk_weight.size]
    qk_total = qk_total.reshape(qk_weight.shape)

    momentum = lax.dynamic_slice(
        head_block_momentum, (jnp.minimum(block, mats - 1), 0, piece * cols), (1, rows, cols)
    )[0]
    moment_wide = momentum_decay * momentum.astype(jnp.float32) + grad_total
    pushed = (grad_total + momentum_decay * moment_wide).astype(jnp.bfloat16)

    pushed = spread(pushed, SHARD).reshape(HEAD, cols)
    pushed = spread(pushed, COLUMNS).transpose(1, 0, 2).reshape(HEAD, width)
    ortho = orthogonalize(pushed)
    energy = slot_energy(ortho, pushed)
    own = lax.dynamic_slice(ortho, (shard * rows, piece * cols), (rows, cols))

    is_mat = block < mats
    energy_high, energy_low = split_wide(energy)
    spare = jnp.arange(SPARE, dtype=jnp.int32)[:, None]
    energies = jnp.broadcast_to(jnp.where(spare == 0, energy_high, energy_low), (SPARE, cols))
    finished = jnp.concatenate(
        [
            jnp.where(is_mat, own, grad_total.astype(jnp.bfloat16)),
            moment_wide.astype(jnp.bfloat16),
            energies,
        ],
        axis=0,
    )
    finished = spread(finished, "y")
    energies = finished[:mats, 2 * rows : 2 * rows + 2, 0].astype(jnp.float32)
    energies = energies[:, 0] + energies[:, 1]
    slots = owner_slots(owners, -(-mats // lax.axis_size(SHARD)))
    owner_sums = jnp.sum(jnp.where(slots == shard, energies, 0.0)).reshape(1, 1)
    finished = jnp.concatenate(
        [finished[:, :rows], finished[:mats, rows : 2 * rows]], axis=0
    )
    finished = spread(finished, COLUMNS).transpose(1, 2, 0, 3)
    finished = finished.reshape(blocks + mats, rows, width)
    new_weight = (
        mat_weight.astype(jnp.float32) * (1.0 - muon_rate * weight_decay)
        - muon_rate * muon_scale * finished[:mats].astype(jnp.float32)
    ).astype(jnp.bfloat16)
    new_moment = finished[blocks:]
    emb_total = finished[mats:blocks].reshape(emb_weight.shape).astype(jnp.float32)
    emb_new, emb_first_new, emb_second_new = adamw(emb_weight, emb_total, emb_first, emb_second)
    norm_new, norm_first_new, norm_second_new = adamw(
        norm_weight, norm_total, norm_first, norm_second
    )
    qk_new, qk_first_new, qk_second_new = adamw(qk_weight, qk_total, qk_first, qk_second)
    return (
        new_weight,
        new_moment,
        owner_sums,
        emb_new,
        emb_first_new,
        emb_second_new,
        norm_new,
        norm_first_new,
        norm_second_new,
        qk_new,
        qk_first_new,
        qk_second_new,
    )


def solution(mesh):
    mesh = Mesh(mesh.devices.reshape(4, 2, 8, 4, 2), ("x", "z_lo", "y", "z_hi", "core"))
    group = ("x", "z_lo", "y")
    placed = (
        P(),
        P(None, SHARD, None),
        P(group, None, SHARD, None),
        P(None, SHARD, None),
        P(SHARD, None),
        P(group, SHARD, None),
        P(SHARD, None),
        P(SHARD, None),
        P(None, SHARD),
        P(group, None, SHARD),
        P(None, SHARD),
        P(None, SHARD),
        P(),
        P(group, None, None),
        P(),
        P(),
    )
    return jax.shard_map(
        on_device,
        mesh=mesh,
        in_specs=placed,
        out_specs=(
            P(None, SHARD, None),
            P(None, SHARD, None),
            P(SHARD, None),
            P(SHARD, None),
            P(SHARD, None),
            P(SHARD, None),
            P(None, SHARD),
            P(None, SHARD),
            P(None, SHARD),
            P(),
            P(),
            P(),
        ),
        check_vma=False,
    )
```

```python
import math

import jax
import jax.numpy as jnp
from jax import lax
from jax.experimental import pallas as pl
from jax.experimental.pallas import tpu as pltpu
from jax.sharding import Mesh, PartitionSpec as P

D = 4096
HEAD = 128
MATS = 6
NS_ITERS = 5


momentum_decay = 0.95
muon_rate = 0.02
weight_decay = 0.1
adam_rate = 0.01
beta_first = 0.9
beta_second = 0.95
adam_epsilon = 1e-08
bias_first = 1.0 - 0.9**10
bias_second = 1.0 - 0.95**10
norm_epsilon = 1e-07
quintic_a = 3.4445
quintic_b = -4.775
quintic_c = 2.0315


COLUMNS = ("x", "z_lo")
SHARD = ("z_hi", "core")
SPARE = 8


def exchange(stacked, axes):
    return lax.all_to_all(stacked, axes, split_axis=0, concat_axis=0, tiled=True)


def spread(piece, axes):
    return exchange(jnp.broadcast_to(piece[None], (lax.axis_size(axes),) + piece.shape), axes)


def split_wide(wide):
    high = lax.reduce_precision(wide, 8, 7)
    low = lax.reduce_precision(wide - high, 8, 7)
    return high.astype(jnp.bfloat16), low.astype(jnp.bfloat16)


def pack(mat_grad, emb_grad, norm_grad, qk_grad, pieces):
    mats, rows, width = mat_grad.shape
    embs = emb_grad.shape[0]
    cols = width // pieces
    taken = mats * rows + embs

    def kernel(mat_ref, emb_ref, norm_ref, qk_ref, out_ref, gains_ref):
        heads = qk_ref.shape[1]
        gains_ref[...] = jnp.zeros_like(gains_ref)
        gains_ref[0:2, :] = norm_ref[...].astype(jnp.float32)
        gains_ref[2:3, 0:heads] = qk_ref[0:1, :].astype(jnp.float32)
        gains_ref[2:3, heads : 2 * heads] = qk_ref[1:2, :].astype(jnp.float32)
        gains = gains_ref[...].astype(jnp.bfloat16)
        for piece in range(pieces):
            span = slice(piece * cols, (piece + 1) * cols)
            for mat in range(mats):
                out_ref[piece, mat * rows : (mat + 1) * rows, :] = mat_ref[mat, :, span]
            out_ref[piece, mats * rows : taken, :] = emb_ref[:, span]
            out_ref[piece, taken : taken + SPARE, :] = gains

    return pl.pallas_call(
        kernel,
        out_shape=jax.ShapeDtypeStruct((pieces, taken + SPARE, cols), jnp.bfloat16),
        scratch_shapes=[pltpu.VMEM((SPARE, cols), jnp.float32)],
        compiler_params=pltpu.CompilerParams(vmem_limit_bytes=8 << 20),
        name="pack",
    )(mat_grad, emb_grad, norm_grad, qk_grad)


def orthogonalize(pushed, held, where, copies):
    pieces, _, cols = pushed.shape
    rows = held.shape[0]
    spans = [slice(piece * cols, (piece + 1) * cols) for piece in range(pieces)]

    def folded(wide):
        return jnp.sum(wide.reshape(HEAD // 8, 8, cols), axis=0)

    def kernel(where_ref, pushed_ref, held_ref, out_ref, iterate_ref, ortho_ref):
        squares = jnp.zeros((8, cols), jnp.float32)
        for piece in range(pieces):
            wide = pushed_ref[piece].astype(jnp.float32)
            squares = squares + folded(wide * wide)
        squares = jnp.sum(jnp.sum(squares, axis=0, keepdims=True), axis=1, keepdims=True)
        inverse = 1.0 / (jnp.sqrt(squares) + norm_epsilon)
        for piece in range(pieces):
            wide = pushed_ref[piece].astype(jnp.float32)
            iterate_ref[:, spans[piece]] = (wide * inverse).astype(jnp.bfloat16)
        energy = jnp.zeros((8, cols), jnp.float32)
        for sweep in range(NS_ITERS):
            iterate = iterate_ref[...]
            gram = lax.dot_general(
                iterate, iterate, (((1,), (1,)), ((), ())), preferred_element_type=jnp.float32
            ).astype(jnp.bfloat16)
            squared = jnp.dot(gram, gram, preferred_element_type=jnp.float32)
            blend = (quintic_b * gram.astype(jnp.float32) + quintic_c * squared).astype(
                jnp.bfloat16
            )
            for piece in range(pieces):
                old = iterate_ref[:, spans[piece]]
                new = (
                    quintic_a * old.astype(jnp.float32)
                    + jnp.dot(blend, old, preferred_element_type=jnp.float32)
                ).astype(jnp.bfloat16)
                if sweep < NS_ITERS - 1:
                    iterate_ref[:, spans[piece]] = new
                else:
                    ortho_ref[piece] = new
                    energy = energy + folded(
                        new.astype(jnp.float32) * pushed_ref[piece].astype(jnp.float32)
                    )
        energy = jnp.sum(jnp.sum(energy, axis=0, keepdims=True), axis=1, keepdims=True)
        energy = energy / (HEAD * math.sqrt(D))
        high = energy.astype(jnp.bfloat16).astype(jnp.float32)
        low = energy - high
        row = lax.broadcasted_iota(jnp.int32, (SPARE, cols), 0)
        energies = jnp.where(row == 0, high, low).astype(jnp.bfloat16)
        start = pl.multiple_of(where_ref[1] * rows, rows)
        own = ortho_ref[where_ref[0], pl.ds(start, rows), :]
        for copy in range(copies):
            out_ref[copy, 0:rows, :] = own
            out_ref[copy, rows : 2 * rows, :] = held_ref[...]
            out_ref[copy, 2 * rows : 2 * rows + SPARE, :] = energies

    return pl.pallas_call(
        kernel,
        out_shape=jax.ShapeDtypeStruct((copies, 2 * rows + SPARE, cols), jnp.bfloat16),
        in_specs=[
            pl.BlockSpec(memory_space=pltpu.SMEM),
            pl.BlockSpec(memory_space=pltpu.VMEM),
            pl.BlockSpec(memory_space=pltpu.VMEM),
        ],
        scratch_shapes=[
            pltpu.VMEM((HEAD, pieces * cols), jnp.bfloat16),
            pltpu.VMEM((pieces, HEAD, cols), jnp.bfloat16),
        ],
        compiler_params=pltpu.CompilerParams(vmem_limit_bytes=12 << 20),
        name="newton_schulz",
    )(where, pushed, held)


def fan_out(finished, mats, rows, copies):
    blocks, _, cols = finished.shape

    def kernel(finished_ref, out_ref):
        for copy in range(copies):
            out_ref[copy, 0:mats] = finished_ref[0:mats, 0:rows, :]
            out_ref[copy, mats : mats + blocks] = finished_ref[:, rows : 2 * rows, :]

    return pl.pallas_call(
        kernel,
        out_shape=jax.ShapeDtypeStruct((copies, mats + blocks, rows, cols), jnp.bfloat16),
        compiler_params=pltpu.CompilerParams(vmem_limit_bytes=8 << 20),
        name="fan_out",
    )(finished)


def owner_slots(owners, capacity):
    order = jnp.arange(owners.shape[0], dtype=jnp.int32)
    same = (owners[:, None] == owners[None, :]) & (order[None, :] < order[:, None])
    position = jnp.sum(same.astype(jnp.int32), axis=1)
    return owners * capacity + position


def adamw(weight, grad_sum, first, second):
    first_new = beta_first * first + (1.0 - beta_first) * grad_sum
    second_new = beta_second * second + (1.0 - beta_second) * grad_sum * grad_sum
    wide_weight = weight.astype(jnp.float32)
    stepped = (
        first_new / bias_first / (jnp.sqrt(second_new / bias_second) + adam_epsilon)
        + weight_decay * wide_weight
    )
    return ((wide_weight - adam_rate * stepped).astype(jnp.bfloat16), first_new, second_new)


def on_device(
    owners,
    mat_weight,
    mat_grad,
    head_block_momentum,
    emb_weight,
    emb_grad,
    emb_first,
    emb_second,
    norm_weight,
    norm_grad,
    norm_first,
    norm_second,
    qk_weight,
    qk_grad,
    qk_first,
    qk_second,
):
    muon_scale = 0.2 * math.sqrt(max(HEAD, D))
    mats, rows, width = mat_weight.shape
    blocks = lax.axis_size("y")
    pieces = lax.axis_size(COLUMNS)
    cols = width // pieces
    block = lax.axis_index("y")
    piece = lax.axis_index(COLUMNS)
    shard = lax.axis_index(SHARD)

    where = jnp.stack([piece, shard]).astype(jnp.int32)
    momentum = lax.dynamic_slice(
        head_block_momentum, (jnp.minimum(block, mats - 1), 0, piece * cols), (1, rows, cols)
    )[0]
    mat_grad, where, momentum, is_mat = lax.optimization_barrier(
        (mat_grad, where, momentum, block < mats)
    )

    outgoing = pack(mat_grad[0], emb_grad[0], norm_grad[0], qk_grad[0], pieces)
    partial = jnp.sum(exchange(outgoing, COLUMNS).astype(jnp.float32), axis=0)

    gains_high, gains_low = split_wide(partial[blocks * rows : blocks * rows + SPARE // 2])
    gains = jnp.concatenate([gains_high, gains_low], axis=0)
    outgoing = jnp.concatenate(
        [
            partial[: blocks * rows].astype(jnp.bfloat16).reshape(blocks, rows, cols),
            jnp.broadcast_to(gains[None], (blocks, SPARE, cols)),
        ],
        axis=1,
    )
    total = jnp.sum(exchange(outgoing, "y").astype(jnp.float32), axis=0)
    grad_total = total[:rows]
    gains = total[rows : rows + SPARE // 2] + total[rows + SPARE // 2 :]
    gains = gains.reshape(-1)
    norm_total = gains[: norm_weight.size].reshape(norm_weight.shape)
    qk_total = gains[norm_weight.size : norm_weight.size + qk_weight.size]
    qk_total = qk_total.reshape(qk_weight.shape)

    moment_wide = momentum_decay * momentum.astype(jnp.float32) + grad_total
    pushed = (grad_total + momentum_decay * moment_wide).astype(jnp.bfloat16)

    held = jnp.where(is_mat, moment_wide, grad_total).astype(jnp.bfloat16)

    pushed = spread(pushed, SHARD).reshape(HEAD, cols)
    pushed = spread(pushed, COLUMNS)

    finished = exchange(orthogonalize(pushed, held, where, blocks), "y")
    energies = finished[:mats, 2 * rows : 2 * rows + 2, 0].astype(jnp.float32)
    energies = energies[:, 0] + energies[:, 1]
    slots = owner_slots(owners, -(-mats // lax.axis_size(SHARD)))
    owner_sums = jnp.sum(jnp.where(slots == shard, energies, 0.0)).reshape(1, 1)
    finished = exchange(fan_out(finished, mats, rows, pieces), COLUMNS)
    finished = finished.transpose(1, 2, 0, 3).reshape(mats + blocks, rows, width)
    ortho = finished[:mats]
    new_moment = finished[mats : 2 * mats]
    emb_total = finished[2 * mats :].reshape(emb_weight.shape).astype(jnp.float32)
    new_weight = (
        mat_weight.astype(jnp.float32) * (1.0 - muon_rate * weight_decay)
        - muon_rate * muon_scale * ortho.astype(jnp.float32)
    ).astype(jnp.bfloat16)
    emb_new, emb_first_new, emb_second_new = adamw(emb_weight, emb_total, emb_first, emb_second)
    norm_new, norm_first_new, norm_second_new = adamw(
        norm_weight, norm_total, norm_first, norm_second
    )
    qk_new, qk_first_new, qk_second_new = adamw(qk_weight, qk_total, qk_first, qk_second)
    return (
        new_weight,
        new_moment,
        owner_sums,
        emb_new,
        emb_first_new,
        emb_second_new,
        norm_new,
        norm_first_new,
        norm_second_new,
        qk_new,
        qk_first_new,
        qk_second_new,
    )


def solution(mesh):
    mesh = Mesh(mesh.devices.reshape(4, 2, 8, 4, 2), ("x", "z_lo", "y", "z_hi", "core"))
    group = ("x", "z_lo", "y")
    placed = (
        P(),
        P(None, SHARD, None),
        P(group, None, SHARD, None),
        P(None, SHARD, None),
        P(SHARD, None),
        P(group, SHARD, None),
        P(SHARD, None),
        P(SHARD, None),
        P(None, SHARD),
        P(group, None, SHARD),
        P(None, SHARD),
        P(None, SHARD),
        P(),
        P(group, None, None),
        P(),
        P(),
    )
    return jax.shard_map(
        on_device,
        mesh=mesh,
        in_specs=placed,
        out_specs=(
            P(None, SHARD, None),
            P(None, SHARD, None),
            P(SHARD, None),
            P(SHARD, None),
            P(SHARD, None),
            P(SHARD, None),
            P(None, SHARD),
            P(None, SHARD),
            P(None, SHARD),
            P(),
            P(),
            P(),
        ),
        check_vma=False,
    )
```
